768 devices in a mesh: dp: 128 (over y, x, z_hi), ctx: 6 (over z_lo, core).
Axes of the slice: x: 4, y: 8, z: 12 (z_hi: 4, z_lo: 3; z = z_hi * 3 + z_lo), core: 2. Of those that a mesh axis runs over, the one named last changes fastest.
Arguments:
- queries: bfloat16 [128, 768, 128], P('dp', 'ctx'), may hold values from -6 to 6
- key_vectors: bfloat16 [128, 768, 128], P('dp', 'ctx'), may hold values from -6 to 6
- value_vectors: bfloat16 [128, 768, 128], P('dp', 'ctx'), may hold values from -6 to 6
- log_decay: float32 [128, 768, 128], P('dp', 'ctx'), may hold values from -2 to 0, as said below
- out_weight: bfloat16 [5120, 128], replicated, may hold values from -0.5 to 0.5
- cotangent: bfloat16 [128, 768, 5120], P('dp', 'ctx'), may hold values from -1.25 to 1.25
Outputs:
- grad_queries: bfloat16 [128, 768, 128], P('dp', 'ctx')
- grad_keys: bfloat16 [128, 768, 128], P('dp', 'ctx')
- grad_values: bfloat16 [128, 768, 128], P('dp', 'ctx')
- grad_decay: float32 [128, 768, 128], P('dp', 'ctx')
- grad_weight: float32 [5120, 128], P('dp')
The draws below stay inside these ranges and needn't reach their ends.
Inputs may be any that keep to these rules, and one draw needn't show every extreme that they name: `log_decay`: every entry is negative.
All inputs are finite; a program needn't handle non-finite values.
Results may differ from the reference program's by a relative error of at most 0.0029.
Values sent between devices are 32-bit elements; how exact they have to be, the bound alone decides.
A program may use at most 32 MiB of HBM per device.

```python
import jax
import jax.numpy as jnp
from jax import lax

D = 5120
DK = 128
HEADS = 1
BLK = 128
TOK_DEV = 128
HK = 128
SEQUENCE_LENGTH = 768
BATCH = 128


def draw_log_decay(key, part):
    subkeys = jax.random.split(jax.random.fold_in(key, 17), 7)
    fast_share = 0.5
    is_fast = jax.random.uniform(subkeys[0], (BATCH, 1, HK)) < fast_share
    fast_rate = jnp.exp(jax.random.uniform(subkeys[1], (BATCH, 1, HK), minval=jnp.log(1.0 / 50.0), maxval=jnp.log(1.0 / 30.0)))
    slow_rate = jnp.exp(jax.random.uniform(subkeys[2], (BATCH, 1, HK), minval=jnp.log(0.05 / SEQUENCE_LENGTH), maxval=jnp.log(0.3 / SEQUENCE_LENGTH)))
    decay_speed = jnp.where(is_fast, fast_rate, slow_rate)
    segments = SEQUENCE_LENGTH // TOK_DEV
    device_multiplier = jnp.exp(jax.random.uniform(subkeys[3], (BATCH, segments, 1, HK), minval=jnp.log(0.5), maxval=jnp.log(2.0)))
    device_multiplier = jnp.broadcast_to(device_multiplier, (BATCH, segments, TOK_DEV, HK)).reshape(BATCH, SEQUENCE_LENGTH, HK)
    token_multiplier = jnp.exp(jax.random.uniform(subkeys[4], (BATCH, SEQUENCE_LENGTH, HK), minval=jnp.log(0.5), maxval=jnp.log(2.0)))
    token_positions = jax.random.randint(subkeys[5], (BATCH, 2, 1), 0, SEQUENCE_LENGTH)
    spike_strength = jax.random.uniform(subkeys[6], (BATCH, 2, 1), minval=jnp.log(0.5), maxval=jnp.log(0.8))
    during_spike = jnp.arange(SEQUENCE_LENGTH)[None, None, :] == token_positions
    spike_log_decay = jnp.sum(jnp.where(during_spike, spike_strength, 0.0), axis=1)[:, :, None]
    return (-decay_speed * device_multiplier * token_multiplier + spike_log_decay).astype(jnp.float32)


def spiked(array, stream_key, source, target, blocks, factor):
    def block_of(axis_at):
        return (jnp.arange(array.shape[axis_at]) // (array.shape[axis_at] // blocks)).reshape((-1,) + (1,) * (array.ndim - 1 - axis_at))

    near = jax.random.permutation(stream_key, blocks)[block_of(target)]
    second = (block_of(target) + blocks // 2) % blocks
    return jnp.where((block_of(source) == near) | (block_of(source) == second), factor * array, array)


def levels(rng, shape, pieces, low, top_value):
    def one(axis_at, parts):
        steps = jax.random.uniform(jax.random.fold_in(jax.random.fold_in(rng, 6), axis_at), (parts,), jnp.float32, low / len(pieces), top_value / len(pieces))
        return jnp.repeat(jnp.exp(steps), shape[axis_at] // parts).reshape((-1,) + (1,) * (len(shape) - axis_at - 1))

    loudness = one(*pieces[0])
    for cut in pieces[1:]:
        loudness = loudness * one(*cut)
    return loudness


def noise(rng, dims, deviation, reach, cuts=(), kind=jnp.bfloat16):
    values = deviation * jax.random.normal(rng, dims, jnp.float32)
    if cuts:
        values = values * levels(rng, dims, cuts, -0.22, 0.18)
    return jnp.clip(values, -reach, reach).astype(kind)


def noise_with(own_key, shape, width, most, pieces, heavy, held_as=jnp.bfloat16):
    array = width * jax.random.normal(own_key, shape, jnp.float32)
    if pieces:
        array = array * levels(own_key, shape, pieces, -0.22, 0.18)
    return jnp.clip(spiked(array, jax.random.fold_in(own_key, 3), *heavy), -most, most).astype(held_as)


def setup_inputs(seed: int = 0) -> dict:
    arg_keys = jax.random.split(jax.random.key(seed), 7)
    return {
        "queries": noise(arg_keys[0], (BATCH, SEQUENCE_LENGTH, HK), 1.0, 6.0, ((0, 128), (1, 6))),
        "key_vectors": noise(arg_keys[1], (BATCH, SEQUENCE_LENGTH, HK), 1.0, 6.0, ((0, 128), (1, 6))),
        "value_vectors": noise(arg_keys[2], (BATCH, SEQUENCE_LENGTH, HK), 1.0, 6.0, ((0, 128), (1, 6))),
        "log_decay": draw_log_decay(jax.random.fold_in(arg_keys[6], 71), 0),
        "out_weight": noise(arg_keys[4], (D, HK), HK ** -0.5, 0.5),
        "cotangent": noise_with(arg_keys[5], (BATCH, SEQUENCE_LENGTH, D), 0.05, 1.25, ((0, 128), (1, 6)), (0, 2, 128, 5.5)),
    }


EPSILON = 1e-05
PRECISE = lax.Precision.HIGHEST

def normalize_heads(output):
    return output * lax.rsqrt(lax.optimization_barrier(jnp.mean(output * output, axis=-1, keepdims=True)) + EPSILON)

def attend(query_rows, key_rows, value_rows, decay_rows):
    blocks = query_rows.shape[0] // BLK
    shaped = (blocks, BLK, HEADS, DK)
    query_blk = query_rows.reshape(shaped)
    key_blk = key_rows.reshape(shaped)
    value_blk = value_rows.reshape(shaped)
    decay_blk = decay_rows.reshape(shaped)
    cumul = jnp.cumsum(decay_blk, axis=1)
    totals = cumul[:, -1]
    query_scaled = query_blk * jnp.exp(cumul)
    key_scaled = key_blk * jnp.exp(-cumul)
    key_to_end = key_blk * jnp.exp(totals[:, None] - cumul)
    causal = jnp.tril(jnp.ones((BLK, BLK), jnp.float32))
    scores = jnp.einsum('nihc,njhc->nhij', query_scaled, key_scaled, precision=PRECISE) * causal
    within = jnp.einsum('nhij,njhe->nihe', scores, value_blk, precision=PRECISE)
    block_states = jnp.einsum('njhc,njhe->nhce', key_to_end, value_blk, precision=PRECISE)

    def advance(carry, inputs):
        block_decay, block_state = inputs
        return (jnp.exp(block_decay)[..., None] * carry + block_state, carry)
    initial = jnp.zeros((HEADS, DK, DK), jnp.float32)
    last_state, entries = lax.scan(advance, initial, (totals, block_states))
    across = jnp.einsum('nihc,nhce->nihe', query_scaled, entries, precision=PRECISE)
    return normalize_heads(within + across).reshape(blocks * BLK, HEADS * DK)

def reference(queries, key_vectors, value_vectors, log_decay, out_weight, cotangent):

    def one_sequence(weight_sum, inputs):
        query_row, key_row, value_row, decay_row, upstream_row = inputs
        normed, pullback = jax.vjp(attend, query_row.astype(jnp.float32), key_row.astype(jnp.float32), value_row.astype(jnp.float32), decay_row)
        grad_normed = jnp.dot(upstream_row, out_weight, preferred_element_type=jnp.float32)
        grad_query, grad_key, grad_value, grad_gate = pullback(grad_normed)
        rounded = normed.astype(jnp.bfloat16)
        contribution = jnp.dot(upstream_row.T, rounded, preferred_element_type=jnp.float32)
        outputs = (grad_query.astype(jnp.bfloat16), grad_key.astype(jnp.bfloat16), grad_value.astype(jnp.bfloat16), grad_gate)
        return (weight_sum + contribution, outputs)
    initial = jnp.zeros((D, HEADS * DK), jnp.float32)
    grad_weight, grads = lax.scan(one_sequence, initial, (queries, key_vectors, value_vectors, log_decay, cotangent))
    return (grads[0], grads[1], grads[2], grads[3], grad_weight)
```

```python
import jax
import jax.numpy as jnp
from jax import lax
from jax.experimental import pallas as pl
from jax.experimental.pallas import tpu as pltpu
from jax.sharding import PartitionSpec as P

X, Y, Z, ZL, ZH = 4, 8, 12, 3, 4
T = 128
C = 128
D = 5120
R = D // (X * Y * ZH)
EPSILON = 1e-05
MESH = pl.DeviceIdType.MESH
F32 = jnp.float32
BF16 = jnp.bfloat16


def mm(a, b, dims=((1,), (0,)), precision=lax.Precision.HIGHEST):
    return lax.dot_general(a, b, (dims, ((), ())), precision=precision, preferred_element_type=F32)


NT = ((1,), (1,))
TN = ((0,), (0,))


class Ring:
    def __init__(self, me, count, device, own, streams, slots, send, recv):
        self.me, self.count, self.device, self.own = me, count, device, own
        self.slots, self.send, self.recv = slots, send, recv
        self.streams, base = [], 0
        for part, sign, hops in streams:
            self.streams.append((part, sign, hops, base))
            base += hops

    def dest(self, stream, turn):
        _, sign, hops, _ = self.streams[stream]
        return lax.rem(self.me + sign * (hops - turn) + self.count, self.count)

    def copy(self, stream, turn):
        part, sign, _, base = self.streams[stream]
        source = self.own(self.dest(stream, 0), part) if turn == 0 else self.slots.at[base + turn - 1]
        return pltpu.make_async_remote_copy(
            src_ref=source,
            dst_ref=self.slots.at[base + turn],
            send_sem=self.send.at[base + turn],
            recv_sem=self.recv.at[base + turn],
            device_id=self.device(sign),
            device_id_type=MESH,
        )

    def start(self, stream):
        self.copy(stream, 0).start()

    def step(self, stream, turn):
        part, _, _, base = self.streams[stream]
        self.copy(stream, turn - 1).wait_recv()
        self.slots[base + turn - 1] += self.own(self.dest(stream, turn), part)[...]
        self.copy(stream, turn).start()

    def finish(self, stream):
        part, _, hops, base = self.streams[stream]
        self.copy(stream, hops - 1).wait_recv()
        self.own(self.me, part)[...] += self.slots[base + hops - 1]

    def drain(self):
        for index, (_, _, hops, _) in enumerate(self.streams):
            for turn in range(hops):
                self.copy(index, turn).wait_send()


def kernel(
    q_hbm, k_hbm, v_hbm, decay_hbm, weight_hbm, cot_hbm,
    gq_ref, gk_ref, gv_ref, gd_ref, gw_ref,
    q_in, k_in, v_in, decay_in, weight_in, cot_in, cot_t, in_sem,
    acc, pair_slots, pair_send, pair_recv,
    x1_slots, x1_send, x1_recv, y1_slots, y1_send, y1_recv,
    x2_slots, x2_send, x2_recv, y2_slots, y2_send, y2_recv,
    z_slots, z_send, z_recv, w_out, w_send, w_recv,
    f_loc, f_mate, f_pair, f_in, f_mate_send, f_mate_recv, f_send, f_recv,
    b_loc, b_mate, b_pair, b_in, b_mate_send, b_mate_recv, b_send, b_recv,
):
    dp, ctx = lax.axis_index("dp"), lax.axis_index("ctx")
    yy = dp // (X * ZH)
    xx = (dp // ZH) % X
    zz = (dp % ZH) * ZL + ctx // 2
    core = ctx % 2
    chip = ctx // 2

    def at(y, x, z, h):
        return {"dp": (y * X + x) * ZH + z // ZL, "ctx": (z % ZL) * 2 + h}

    def near_x(sign):
        return at(yy, lax.rem(xx + sign + X, X), zz, core)

    def near_y(sign):
        return at(lax.rem(yy + sign + Y, Y), xx, zz, core)

    mate = at(yy, xx, zz, 1 - core)
    base_z = 6 * core
    gathers = zz // 6 == core

    operands = (
        (decay_hbm, decay_in), (k_hbm, k_in), (v_hbm, v_in), (q_hbm, q_in), (cot_hbm, cot_in), (weight_hbm, weight_in),
    )
    loads = [pltpu.make_async_copy(a, b, in_sem.at[i]) for i, (a, b) in enumerate(operands)]
    for load in loads:
        load.start()

    barrier = pltpu.get_barrier_semaphore()

    def greet(device):
        pl.semaphore_signal(barrier, inc=1, device_id=device, device_id_type=MESH)

    @pl.when(gathers)
    def _():
        for far in (6, 5, 7, 4, 8, 3, 9, 2, 10, 1, 11):
            greet(at(yy, xx, lax.rem(zz + far, Z), core))

    @pl.when(jnp.logical_not(gathers))
    def _():
        for i in range(6):
            greet(at(yy, xx, base_z + i, core))

    for sign in (1, -1):
        greet(near_y(sign))
        greet(near_x(sign))
    for step in range(1, 6):
        greet({"dp": dp, "ctx": lax.rem(ctx + step, 6)})

    row = lax.broadcasted_iota(jnp.int32, (T, T), 0)
    column = lax.broadcasted_iota(jnp.int32, (T, T), 1)
    lower = (row >= column).astype(F32)
    loads[0].wait()
    cumul = mm(lower, decay_in[...])
    total = cumul[T - 1 : T, :]
    decay = jnp.exp(total)
    loads[1].wait()
    loads[2].wait()
    key = k_in[...].astype(F32)
    value = v_in[...].astype(F32)
    key_to_end = key * jnp.exp(total - cumul)
    local = mm(value, key_to_end, TN)
    f_loc[:C, :] = local
    f_loc[C:, :] = jnp.broadcast_to(decay, (8, C))

    @pl.when(gathers)
    def _():
        pl.semaphore_wait(barrier, 20)

    @pl.when(jnp.logical_not(gathers))
    def _():
        pl.semaphore_wait(barrier, 15)

    def far_sends(pair, slots, send, recv, first, last):
        def copy(slot, target, h, index):
            return pltpu.make_async_remote_copy(
                pair, slots.at[slot], send.at[index], recv.at[slot],
                device_id={"dp": dp, "ctx": 2 * target + h}, device_id_type=MESH,
            )

        from_first = [copy(0, last, h, h) for h in (0, 1)] + [copy(0, 1, h, 2 + h) for h in (0, 1)]
        from_middle = [copy(1, last, h, h) for h in (0, 1)]
        return from_first, from_middle

    f_first, f_middle = far_sends(f_pair, f_in, f_send, f_recv, 0, 2)
    b_first, b_middle = far_sends(b_pair, b_in, b_send, b_recv, 2, 0)
    f_to_mate = pltpu.make_async_remote_copy(
        f_loc, f_mate, f_mate_send, f_mate_recv, device_id=mate, device_id_type=MESH
    )
    b_to_mate = pltpu.make_async_remote_copy(
        b_loc, b_mate, b_mate_send, b_mate_recv, device_id=mate, device_id_type=MESH
    )
    even = core == 0
    odd = core == 1

    @pl.when(even)
    def _():
        f_to_mate.start()

    loads[3].wait()
    query = q_in[...].astype(F32)
    rising = jnp.exp(cumul)
    falling = jnp.exp(-cumul)
    query_scaled = query * rising
    key_scaled = key * falling
    scores = mm(query_scaled, key_scaled, NT) * lower

    @pl.when(odd)
    def _():
        f_to_mate.wait_recv()
        f_pair[:C, :] = f_loc[C : C + 1, :] * f_mate[:C, :] + f_loc[:C, :]
        f_pair[C:, :] = f_loc[C:, :] * f_mate[C:, :]

        @pl.when(chip == 0)
        def _():
            for copy in f_first:
                copy.start()

        @pl.when(chip == 1)
        def _():
            for copy in f_middle:
                copy.start()

    within = mm(scores, value)
    loads[4].wait()
    for i in range(D // 128):
        cot_t[128 * i : 128 * (i + 1), :] = cot_in[:, 128 * i : 128 * (i + 1)].T
    loads[5].wait()
    grad_normed = jnp.dot(cot_in[...], weight_in[...], preferred_element_type=F32)

    def carried(slots, copies_first, copies_middle, here_first, here_last, loc_in):
        @pl.when(chip == here_first)
        def _():
            loc_in[...] = jnp.zeros_like(loc_in)

        @pl.when(chip == 1)
        def _():
            copies_first[0].wait_recv()
            loc_in[...] = slots[0, :C, :]

        @pl.when(chip == here_last)
        def _():
            copies_first[0].wait_recv()
            copies_middle[0].wait_recv()
            loc_in[...] = slots[1, C : C + 1, :] * slots[0, :C, :] + slots[1, :C, :]

    state_ref = w_out.at[0:C]
    carried(f_in, f_first, f_middle, 0, 2, state_ref)

    @pl.when(odd)
    def _():
        state_ref[...] = f_mate[C : C + 1, :] * state_ref[...] + f_mate[:C, :]

    state_in = state_ref[...]
    output = within + mm(query_scaled, state_in, NT)
    scale_inv = lax.rsqrt(jnp.mean(output * output, axis=-1, keepdims=True) + EPSILON)
    normed = output * scale_inv
    rounded = normed.astype(BF16)

    mine, theirs = 2 * core, 2 * (1 - core)
    x_order = (2, 1, 3, 0)
    y_order = (4, 3, 5, 2, 6, 1, 7, 0)

    def x_pair(k):
        there = lax.rem(xx + x_order[k], X)
        return there, pltpu.make_async_remote_copy(
            acc.at[:, there, theirs],
            pair_slots.at[0, :, there],
            pair_send.at[k],
            pair_recv.at[k],
            device_id=mate,
            device_id_type=MESH,
        )

    def y_pair(k):
        there = lax.rem(yy + y_order[k], Y)
        return there, pltpu.make_async_remote_copy(
            acc.at[there, :, theirs + 1],
            pair_slots.at[1, there],
            pair_send.at[X + k],
            pair_recv.at[X + k],
            device_id=mate,
            device_id_type=MESH,
        )

    for k in range(X):
        there, copy = x_pair(k)
        for y in range(Y):
            rows = pl.ds(pl.multiple_of((y * X + there) * (ZH * R), 32), ZH * R)
            share = jnp.dot(cot_t[rows, :], rounded, preferred_element_type=F32)
            acc[y, there] = share.reshape(ZH, R, C)
        copy.start()
    for k in range(Y):
        y_pair(k)[1].start()

    grad_output = scale_inv * (grad_normed - normed * jnp.mean(grad_normed * normed, axis=-1, keepdims=True))
    b_loc[:C, :] = mm(grad_output, query_scaled, TN)
    b_loc[C:, :] = jnp.broadcast_to(decay, (8, C))

    @pl.when(odd)
    def _():
        b_to_mate.start()

    x1 = Ring(
        xx, X, near_x, lambda dest, part: acc.at[4 * part : 4 * part + 4, dest, mine],
        ((0, 1, 2), (1, -1, 2), (1, 1, 1), (0, -1, 1)), x1_slots, x1_send, x1_recv,
    )
    y1 = Ring(
        yy, Y, near_y, lambda dest, part: acc.at[dest, 2 * part : 2 * part + 2, mine + 1],
        ((0, 1, 4), (1, -1, 4), (1, 1, 3), (0, -1, 3)), y1_slots, y1_send, y1_recv,
    )
    x2 = Ring(
        yy, Y, near_y, lambda dest, part: acc.at[dest, xx, mine],
        ((0, 1, 4), (0, -1, 3)), x2_slots, x2_send, x2_recv,
    )
    y2 = Ring(
        xx, X, near_x, lambda dest, part: acc.at[yy, dest, mine + 1],
        ((0, 1, 2), (0, -1, 1)), y2_slots, y2_send, y2_recv,
    )

    def take_x(k):
        there, copy = x_pair(k)
        copy.wait_recv()
        acc[:, there, mine] += pair_slots[0, :, there]

    def take_y(k):
        there, copy = y_pair(k)
        copy.wait_recv()
        acc[there, :, mine + 1] += pair_slots[1, there]

    take_x(0)
    x1.start(0)
    x1.start(1)
    take_x(1)
    x1.start(2)
    take_x(2)
    x1.start(3)
    take_x(3)
    take_y(0)
    y1.start(0)
    y1.start(1)
    take_y(1)
    y1.start(2)
    take_y(2)
    y1.start(3)
    for k in range(3, Y):
        take_y(k)

    @pl.when(even)
    def _():
        b_to_mate.wait_recv()
        b_pair[:C, :] = b_loc[C : C + 1, :] * b_mate[:C, :] + b_loc[:C, :]
        b_pair[C:, :] = b_loc[C:, :] * b_mate[C:, :]

        @pl.when(chip == 2)
        def _():
            for copy in b_first:
                copy.start()

        @pl.when(chip == 1)
        def _():
            for copy in b_middle:
                copy.start()

    y1.step(0, 1)
    y1.step(1, 1)
    x1.step(0, 1)
    x1.step(1, 1)
    y1.step(2, 1)
    y1.step(3, 1)
    pairs = mm(grad_output, value, NT) * lower
    grad_query = rising * (mm(pairs, key_scaled) + mm(grad_output, state_in))
    gq_ref[...] = grad_query.astype(BF16)
    y1.step(0, 2)
    y1.step(1, 2)
    y1.step(2, 2)
    y1.step(3, 2)
    for stream in range(4):
        x1.finish(stream)
    x2.start(0)
    x2.start(1)
    grad_key = falling * mm(pairs, query_scaled, TN)
    y1.step(0, 3)
    y1.step(1, 3)
    x2.step(0, 1)
    x2.step(1, 1)
    grad_value = mm(scores, grad_output, TN)
    for stream in range(4):
        y1.finish(stream)
    y2.start(0)
    y2.start(1)
    x2.step(0, 2)
    x2.step(1, 2)

    later_ref = w_out.at[0:C]
    carried(b_in, b_first, b_middle, 2, 0, later_ref)

    @pl.when(even)
    def _():
        later_ref[...] = b_mate[C : C + 1, :] * later_ref[...] + b_mate[:C, :]

    later = later_ref[...]
    y2.step(0, 1)
    x2.step(0, 3)
    grad_key += jnp.exp(total - cumul) * mm(value, later)
    gk_ref[...] = grad_key.astype(BF16)
    y2.finish(0)
    y2.finish(1)

    def z_copy(i):
        part = 0 if i < ZL else 1
        return pltpu.make_async_remote_copy(
            acc.at[yy, xx, mine + part],
            z_slots.at[zz],
            z_send.at[i],
            z_recv.at[zz],
            device_id=at(yy, xx, base_z + i, core),
            device_id_type=MESH,
        )

    def z_each(which, act):
        for i in which:

            @pl.when(base_z + i != zz)
            def _():
                act(z_copy(i))

    z_each(range(ZL, 2 * ZL), lambda copy: copy.start())
    x2.finish(0)
    x2.finish(1)
    z_each(range(ZL), lambda copy: copy.start())

    grad_value += mm(key_to_end, later, NT)
    gv_ref[...] = grad_value.astype(BF16)
    gate = query * grad_query - key * grad_key
    end_state = local + decay * state_in
    later_sum = jnp.sum(end_state * later, axis=0, keepdims=True)
    gd_ref[...] = mm(lower, gate, TN) + later_sum

    to_mate = pltpu.make_async_remote_copy(
        w_out.at[C : C + R], w_out.at[C + R :], w_send, w_recv, device_id=mate, device_id_type=MESH
    )

    @pl.when(gathers)
    def _():
        z_slots[zz] = acc[yy, xx, zz // ZL]
        for i in range(Z):

            @pl.when(zz != i)
            def _():
                pltpu.make_async_remote_copy(
                    z_slots.at[i], z_slots.at[i], z_send.at[0], z_recv.at[i], device_id=mate, device_id_type=MESH
                ).wait_recv()

        summed = z_slots[0]
        for i in range(1, Z):
            summed += z_slots[i]
        w_out[C : C + R, :] = summed
        to_mate.start()
        gw_ref[...] = summed
        to_mate.wait_send()

    @pl.when(jnp.logical_not(gathers))
    def _():
        to_mate.wait_recv()
        gw_ref[...] = w_out[C + R :, :]

    z_each(range(2 * ZL), lambda copy: copy.wait_send())
    for k in range(X):
        x_pair(k)[1].wait_send()
    for k in range(Y):
        y_pair(k)[1].wait_send()
    for ring in (x1, y1, x2, y2):
        ring.drain()

    @pl.when(even)
    def _():
        f_to_mate.wait_send()

        @pl.when(chip == 2)
        def _():
            for copy in b_first:
                copy.wait_send()

        @pl.when(chip == 1)
        def _():
            for copy in b_middle:
                copy.wait_send()

    @pl.when(odd)
    def _():
        b_to_mate.wait_send()

        @pl.when(chip == 0)
        def _():
            for copy in f_first:
                copy.wait_send()

        @pl.when(chip == 1)
        def _():
            for copy in f_middle:
                copy.wait_send()


def body(queries, key_vectors, value_vectors, log_decay, out_weight, cotangent):
    vmem, dma = pltpu.VMEM, pltpu.SemaphoreType.DMA

    def slots(count, *block):
        return [vmem((count, *block, R, C), F32), dma((count,)), dma((count,))]

    carried = [vmem((C + 8, C), F32)] * 3 + [vmem((2, C + 8, C), F32), dma, dma, dma((4,)), dma((2,))]
    outs = pl.pallas_call(
        kernel,
        out_shape=[jax.ShapeDtypeStruct((T, C), BF16)] * 3
        + [jax.ShapeDtypeStruct((T, C), F32), jax.ShapeDtypeStruct((R, C), F32)],
        in_specs=[pl.BlockSpec(memory_space=pl.ANY)] * 6,
        out_specs=[pl.BlockSpec(memory_space=pltpu.VMEM)] * 5,
        scratch_shapes=[vmem((T, C), BF16)] * 3
        + [vmem((T, C), F32), vmem((D, C), BF16), vmem((T, D), BF16), vmem((D, T), BF16), dma((6,))]
        + [vmem((Y, X, ZH, R, C), F32), vmem((2, Y, X, R, C), F32), dma((X + Y,)), dma((X + Y,))]
        + slots(6, 4) + slots(14, 2) + slots(7) + slots(3)
        + [vmem((Z, R, C), F32), dma((6,)), dma((Z,)), vmem((C + 2 * R, C), F32), dma, dma]
        + carried + carried,
        compiler_params=pltpu.CompilerParams(
            collective_id=0, has_side_effects=True, vmem_limit_bytes=60 * 1024 * 1024
        ),
    )(queries[0], key_vectors[0], value_vectors[0], log_decay[0], out_weight, cotangent[0])
    return tuple(out[None] for out in outs[:4]) + (outs[4],)


def solution(mesh):
    rows = P("dp", "ctx", None)
    return jax.shard_map(
        body,
        mesh=mesh,
        in_specs=(rows, rows, rows, rows, P(), rows),
        out_specs=(rows, rows, rows, rows, P("dp", None)),
        check_vma=False,
    )
```

```python
import jax
import jax.numpy as jnp
from jax import lax
from jax.experimental import pallas as pl
from jax.experimental.pallas import tpu as pltpu
from jax.sharding import PartitionSpec as P

X, Y, Z, ZL, ZH = 4, 8, 12, 3, 4
T = 128
C = 128
D = 5120
R = D // (X * Y * ZH)
EPSILON = 1e-05
MESH = pl.DeviceIdType.MESH
F32 = jnp.float32
BF16 = jnp.bfloat16
RESULTS = [((T, C), BF16)] * 3 + [((T, C), F32), ((R, C), F32)]


def mm(a, b, dims=((1,), (0,)), precision=lax.Precision.HIGHEST):
    return lax.dot_general(a, b, (dims, ((), ())), precision=precision, preferred_element_type=F32)


NT = ((1,), (1,))
TN = ((0,), (0,))


class Ring:
    def __init__(self, me, count, device, own, streams, slots, send, recv):
        self.me, self.count, self.device, self.own = me, count, device, own
        self.slots, self.send, self.recv = slots, send, recv
        self.streams, base = [], 0
        for part, sign, hops in streams:
            self.streams.append((part, sign, hops, base))
            base += hops

    def dest(self, stream, turn):
        _, sign, hops, _ = self.streams[stream]
        return lax.rem(self.me + sign * (hops - turn) + self.count, self.count)

    def copy(self, stream, turn):
        part, sign, _, base = self.streams[stream]
        source = self.own(self.dest(stream, 0), part) if turn == 0 else self.slots.at[base + turn - 1]
        return pltpu.make_async_remote_copy(
            src_ref=source,
            dst_ref=self.slots.at[base + turn],
            send_sem=self.send.at[base + turn],
            recv_sem=self.recv.at[base + turn],
            device_id=self.device(sign),
            device_id_type=MESH,
        )

    def start(self, stream):
        self.copy(stream, 0).start()

    def step(self, stream, turn):
        part, _, _, base = self.streams[stream]
        self.copy(stream, turn - 1).wait_recv()
        self.slots[base + turn - 1] += self.own(self.dest(stream, turn), part)[...]
        self.copy(stream, turn).start()

    def finish(self, stream):
        part, _, hops, base = self.streams[stream]
        self.copy(stream, hops - 1).wait_recv()
        self.own(self.me, part)[...] += self.slots[base + hops - 1]

    def drain(self):
        for index, (_, _, hops, _) in enumerate(self.streams):
            for turn in range(hops):
                self.copy(index, turn).wait_send()


class Direct:
    def __init__(self, me, count, device, own, order, slots, send, recv):
        self.me, self.count, self.device, self.own, self.order = me, count, device, own, order
        self.slots, self.send, self.recv = slots, send, recv

    def copy(self, index):
        step = self.order[index]
        return pltpu.make_async_remote_copy(
            src_ref=self.own(lax.rem(self.me + step, self.count)),
            dst_ref=self.slots.at[index],
            send_sem=self.send.at[index],
            recv_sem=self.recv.at[index],
            device_id=self.device(step),
            device_id_type=MESH,
        )

    def start(self):
        for index in range(len(self.order)):
            self.copy(index).start()

    def finish(self):
        total = self.own(self.me)[...]
        for index in reversed(range(len(self.order))):
            self.copy(index).wait_recv()
            total += self.slots[index]
        self.own(self.me)[...] = total

    def drain(self):
        for index in range(len(self.order)):
            self.copy(index).wait_send()


def kernel(
    q_hbm, k_hbm, v_hbm, decay_hbm, weight_hbm, cot_hbm,
    gq_ref, gk_ref, gv_ref, gd_ref, gw_ref,
    q_in, k_in, v_in, decay_in, weight_in, cot_in, cot_t, in_sem,
    acc, pair_slots, pair_send, pair_recv,
    x1_slots, x1_send, x1_recv, y1_slots, y1_send, y1_recv,
    x2_slots, x2_send, x2_recv, y2_slots, y2_send, y2_recv,
    z_slots, z_send, z_recv, w_out, w_send, w_recv,
    f_loc, f_mate, f_pair, f_in, f_mate_send, f_mate_recv, f_send, f_recv,
    b_loc, b_mate, b_pair, b_in, b_mate_send, b_mate_recv, b_send, b_recv,
):
    dp, ctx = lax.axis_index("dp"), lax.axis_index("ctx")
    yy = dp // (X * ZH)
    xx = (dp // ZH) % X
    zz = (dp % ZH) * ZL + ctx // 2
    core = ctx % 2
    chip = ctx // 2

    def at(y, x, z, h):
        return {"dp": (y * X + x) * ZH + z // ZL, "ctx": (z % ZL) * 2 + h}

    def near_x(sign):
        return at(yy, lax.rem(xx + sign + X, X), zz, core)

    def near_y(sign):
        return at(lax.rem(yy + sign + Y, Y), xx, zz, core)

    mate = at(yy, xx, zz, 1 - core)
    base_z = 6 * core
    gathers = zz // 6 == core

    operands = (
        (decay_hbm, decay_in), (k_hbm, k_in), (v_hbm, v_in), (q_hbm, q_in), (cot_hbm, cot_in), (weight_hbm, weight_in),
    )
    loads = [pltpu.make_async_copy(a, b, in_sem.at[i]) for i, (a, b) in enumerate(operands)]
    for load in loads:
        load.start()

    barrier = pltpu.get_barrier_semaphore()

    def greet(device):
        pl.semaphore_signal(barrier, inc=1, device_id=device, device_id_type=MESH)

    @pl.when(gathers)
    def _():
        for far in (6, 5, 7, 4, 8, 3, 9, 2, 10, 1, 11):
            greet(at(yy, xx, lax.rem(zz + far, Z), core))

    @pl.when(jnp.logical_not(gathers))
    def _():
        for i in range(6):
            greet(at(yy, xx, base_z + i, core))

    for step in (4, 3, 5, 2, 6, 1, 7):
        greet(near_y(step))
    for step in (2, 1, 3):
        greet(near_x(step))
    for step in range(1, 6):
        greet({"dp": dp, "ctx": lax.rem(ctx + step, 6)})

    row = lax.broadcasted_iota(jnp.int32, (T, T), 0)
    column = lax.broadcasted_iota(jnp.int32, (T, T), 1)
    lower = (row >= column).astype(F32)
    loads[0].wait()
    cumul = mm(lower, decay_in[...])
    total = cumul[T - 1 : T, :]
    decay = jnp.exp(total)
    loads[1].wait()
    loads[2].wait()
    key = k_in[...].astype(F32)
    value = v_in[...].astype(F32)
    key_to_end = key * jnp.exp(total - cumul)
    local = mm(value, key_to_end, TN)
    f_loc[:C, :] = local
    f_loc[C:, :] = jnp.broadcast_to(decay, (8, C))

    @pl.when(gathers)
    def _():
        pl.semaphore_wait(barrier, 26)

    @pl.when(jnp.logical_not(gathers))
    def _():
        pl.semaphore_wait(barrier, 21)

    def far_sends(pair, slots, send, recv, first, last):
        def copy(slot, target, h, index):
            return pltpu.make_async_remote_copy(
                pair, slots.at[slot], send.at[index], recv.at[slot],
                device_id={"dp": dp, "ctx": 2 * target + h}, device_id_type=MESH,
            )

        from_first = [copy(0, last, h, h) for h in (0, 1)] + [copy(0, 1, h, 2 + h) for h in (0, 1)]
        from_middle = [copy(1, last, h, h) for h in (0, 1)]
        return from_first, from_middle

    f_first, f_middle = far_sends(f_pair, f_in, f_send, f_recv, 0, 2)
    b_first, b_middle = far_sends(b_pair, b_in, b_send, b_recv, 2, 0)
    f_to_mate = pltpu.make_async_remote_copy(
        f_loc, f_mate, f_mate_send, f_mate_recv, device_id=mate, device_id_type=MESH
    )
    b_to_mate = pltpu.make_async_remote_copy(
        b_loc, b_mate, b_mate_send, b_mate_recv, device_id=mate, device_id_type=MESH
    )
    even = core == 0
    odd = core == 1

    @pl.when(even)
    def _():
        f_to_mate.start()

    loads[3].wait()
    query = q_in[...].astype(F32)
    rising = jnp.exp(cumul)
    falling = jnp.exp(-cumul)
    query_scaled = query * rising
    key_scaled = key * falling
    scores = mm(query_scaled, key_scaled, NT) * lower

    @pl.when(odd)
    def _():
        f_to_mate.wait_recv()
        f_pair[:C, :] = f_loc[C : C + 1, :] * f_mate[:C, :] + f_loc[:C, :]
        f_pair[C:, :] = f_loc[C:, :] * f_mate[C:, :]

        @pl.when(chip == 0)
        def _():
            for copy in f_first:
                copy.start()

        @pl.when(chip == 1)
        def _():
            for copy in f_middle:
                copy.start()

    within = mm(scores, value)
    loads[4].wait()
    for i in range(D // 128):
        cot_t[128 * i : 128 * (i + 1), :] = cot_in[:, 128 * i : 128 * (i + 1)].T
    loads[5].wait()
    grad_normed = jnp.dot(cot_in[...], weight_in[...], preferred_element_type=F32)

    def carried(slots, copies_first, copies_middle, here_first, here_last, loc_in):
        @pl.when(chip == here_first)
        def _():
            loc_in[...] = jnp.zeros_like(loc_in)

        @pl.when(chip == 1)
        def _():
            copies_first[0].wait_recv()
            loc_in[...] = slots[0, :C, :]

        @pl.when(chip == here_last)
        def _():
            copies_first[0].wait_recv()
            copies_middle[0].wait_recv()
            loc_in[...] = slots[1, C : C + 1, :] * slots[0, :C, :] + slots[1, :C, :]

    state_ref = w_out.at[0:C]
    carried(f_in, f_first, f_middle, 0, 2, state_ref)

    @pl.when(odd)
    def _():
        state_ref[...] = f_mate[C : C + 1, :] * state_ref[...] + f_mate[:C, :]

    state_in = state_ref[...]
    output = within + mm(query_scaled, state_in, NT)
    scale_inv = lax.rsqrt(jnp.mean(output * output, axis=-1, keepdims=True) + EPSILON)
    normed = output * scale_inv
    rounded = normed.astype(BF16)

    mine, theirs = 2 * core, 2 * (1 - core)
    x_order = (2, 1, 3, 0)
    y_order = (4, 3, 5, 2, 6, 1, 7, 0)

    def x_pair(k):
        there = lax.rem(xx + x_order[k], X)
        return there, pltpu.make_async_remote_copy(
            acc.at[:, there, theirs],
            pair_slots.at[0, :, there],
            pair_send.at[k],
            pair_recv.at[k],
            device_id=mate,
            device_id_type=MESH,
        )

    def y_pair(k):
        there = lax.rem(yy + y_order[k], Y)
        return there, pltpu.make_async_remote_copy(
            acc.at[there, :, theirs + 1],
            pair_slots.at[1, there],
            pair_send.at[X + k],
            pair_recv.at[X + k],
            device_id=mate,
            device_id_type=MESH,
        )

    for k in range(X):
        there, copy = x_pair(k)
        for y in range(Y):
            rows = pl.ds(pl.multiple_of((y * X + there) * (ZH * R), 32), ZH * R)
            share = jnp.dot(cot_t[rows, :], rounded, preferred_element_type=F32)
            acc[y, there] = share.reshape(ZH, R, C)
        if k == 0:
            copy.start()
    halves = (("y", 0), ("x", 1), ("y", 1), ("y", 2), ("x", 2), ("x", 3)) + tuple(("y", k) for k in range(3, Y))
    for axis, k in halves:
        (x_pair if axis == "x" else y_pair)(k)[1].start()

    grad_output = scale_inv * (grad_normed - normed * jnp.mean(grad_normed * normed, axis=-1, keepdims=True))
    b_loc[:C, :] = mm(grad_output, query_scaled, TN)
    b_loc[C:, :] = jnp.broadcast_to(decay, (8, C))

    @pl.when(odd)
    def _():
        b_to_mate.start()

    x1 = Ring(
        xx, X, near_x, lambda dest, part: acc.at[4 * part : 4 * part + 4, dest, mine],
        ((0, 1, 2), (1, -1, 2), (1, 1, 1), (0, -1, 1)), x1_slots, x1_send, x1_recv,
    )
    y1 = Ring(
        yy, Y, near_y, lambda dest, part: acc.at[dest, 2 * part : 2 * part + 2, mine + 1],
        ((0, 1, 4), (1, -1, 4), (1, 1, 3), (0, -1, 3)), y1_slots, y1_send, y1_recv,
    )
    x2 = Direct(yy, Y, near_y, lambda dest: acc.at[dest, xx, mine], (4, 3, 5, 2, 6, 1, 7), x2_slots, x2_send, x2_recv)
    y2 = Direct(xx, X, near_x, lambda dest: acc.at[yy, dest, mine + 1], (2, 1, 3), y2_slots, y2_send, y2_recv)

    def take_x(k):
        there, copy = x_pair(k)
        copy.wait_recv()
        acc[:, there, mine] += pair_slots[0, :, there]

    def take_y(k):
        there, copy = y_pair(k)
        copy.wait_recv()
        acc[there, :, mine + 1] += pair_slots[1, there]

    take_x(0)
    x1.start(0)
    x1.start(1)
    take_y(0)
    y1.start(0)
    y1.start(1)
    take_x(1)
    x1.start(2)
    take_y(1)
    y1.start(2)
    take_y(2)
    y1.start(3)
    take_x(2)
    x1.start(3)
    take_x(3)
    for k in range(3, Y):
        take_y(k)

    @pl.when(even)
    def _():
        b_to_mate.wait_recv()
        b_pair[:C, :] = b_loc[C : C + 1, :] * b_mate[:C, :] + b_loc[:C, :]
        b_pair[C:, :] = b_loc[C:, :] * b_mate[C:, :]

        @pl.when(chip == 2)
        def _():
            for copy in b_first:
                copy.start()

        @pl.when(chip == 1)
        def _():
            for copy in b_middle:
                copy.start()

    y1.step(0, 1)
    y1.step(1, 1)
    x1.step(0, 1)
    x1.step(1, 1)
    y1.step(2, 1)
    y1.step(3, 1)
    pairs = mm(grad_output, value, NT) * lower
    y1.step(0, 2)
    y1.step(1, 2)
    grad_query = rising * (mm(pairs, key_scaled) + mm(grad_output, state_in))
    gq_ref[...] = grad_query.astype(BF16)
    y1.step(2, 2)
    y1.step(3, 2)
    for stream in (2, 3, 0, 1):
        x1.finish(stream)
    x2.start()
    y1.step(0, 3)
    y1.step(1, 3)
    grad_key = falling * mm(pairs, query_scaled, TN)
    for stream in (2, 3, 0, 1):
        y1.finish(stream)
    y2.start()
    grad_value = mm(scores, grad_output, TN)

    later_ref = w_out.at[0:C]
    carried(b_in, b_first, b_middle, 2, 0, later_ref)

    @pl.when(even)
    def _():
        later_ref[...] = b_mate[C : C + 1, :] * later_ref[...] + b_mate[:C, :]

    later = later_ref[...]
    grad_key += jnp.exp(total - cumul) * mm(value, later)
    gk_ref[...] = grad_key.astype(BF16)
    x2.finish()

    def z_copy(i):
        part = 0 if i < ZL else 1
        return pltpu.make_async_remote_copy(
            acc.at[yy, xx, mine + part],
            z_slots.at[zz],
            z_send.at[i],
            z_recv.at[zz],
            device_id=at(yy, xx, base_z + i, core),
            device_id_type=MESH,
        )

    def z_each(which, act):
        for i in which:

            @pl.when(base_z + i != zz)
            def _():
                act(z_copy(i))

    z_each(range(ZL), lambda copy: copy.start())
    y2.finish()
    z_each(range(ZL, 2 * ZL), lambda copy: copy.start())

    grad_value += mm(key_to_end, later, NT)
    gv_ref[...] = grad_value.astype(BF16)
    gate = query * grad_query - key * grad_key
    end_state = local + decay * state_in
    later_sum = jnp.sum(end_state * later, axis=0, keepdims=True)
    gd_ref[...] = mm(lower, gate, TN) + later_sum

    to_mate = pltpu.make_async_remote_copy(
        w_out.at[C : C + R], w_out.at[C + R :], w_send, w_recv, device_id=mate, device_id_type=MESH
    )

    @pl.when(gathers)
    def _():
        z_slots[zz] = acc[yy, xx, zz // ZL]
        for i in range(Z):

            @pl.when(zz != i)
            def _():
                pltpu.make_async_remote_copy(
                    z_slots.at[i], z_slots.at[i], z_send.at[0], z_recv.at[i], device_id=mate, device_id_type=MESH
                ).wait_recv()

        summed = z_slots[0]
        for i in range(1, Z):
            summed += z_slots[i]
        w_out[C : C + R, :] = summed
        to_mate.start()
        gw_ref[...] = summed
        to_mate.wait_send()

    @pl.when(jnp.logical_not(gathers))
    def _():
        to_mate.wait_recv()
        gw_ref[...] = w_out[C + R :, :]

    z_each(range(2 * ZL), lambda copy: copy.wait_send())
    for k in range(X):
        x_pair(k)[1].wait_send()
    for k in range(Y):
        y_pair(k)[1].wait_send()
    for ring in (x1, y1, x2, y2):
        ring.drain()

    @pl.when(even)
    def _():
        f_to_mate.wait_send()

        @pl.when(chip == 2)
        def _():
            for copy in b_first:
                copy.wait_send()

        @pl.when(chip == 1)
        def _():
            for copy in b_middle:
                copy.wait_send()

    @pl.when(odd)
    def _():
        b_to_mate.wait_send()

        @pl.when(chip == 0)
        def _():
            for copy in f_first:
                copy.wait_send()

        @pl.when(chip == 1)
        def _():
            for copy in f_middle:
                copy.wait_send()


def store(*refs):
    copies = [pltpu.make_async_copy(refs[i], refs[5 + i], refs[10].at[i]) for i in range(5)]
    for copy in copies:
        copy.start()
    for copy in copies:
        copy.wait()


def body(queries, key_vectors, value_vectors, log_decay, out_weight, cotangent):
    vmem, dma = pltpu.VMEM, pltpu.SemaphoreType.DMA

    def slots(count, *block):
        return [vmem((count, *block, R, C), F32), dma((count,)), dma((count,))]

    carried = [vmem((C + 8, C), F32)] * 3 + [vmem((2, C + 8, C), F32), dma, dma, dma((4,)), dma((2,))]
    outs = pl.pallas_call(
        kernel,
        out_shape=[pltpu.VMEM(shape, dtype) for shape, dtype in RESULTS],
        in_specs=[pl.BlockSpec(memory_space=pltpu.HBM)] * 6,
        out_specs=[pl.BlockSpec(memory_space=pltpu.VMEM)] * 5,
        scratch_shapes=[vmem((T, C), BF16)] * 3
        + [vmem((T, C), F32), vmem((D, C), BF16), vmem((T, D), BF16), vmem((D, T), BF16), dma((6,))]
        + [vmem((Y, X, ZH, R, C), F32), vmem((2, Y, X, R, C), F32), dma((X + Y,)), dma((X + Y,))]
        + slots(6, 4) + slots(14, 2) + slots(7) + slots(3)
        + [vmem((Z, R, C), F32), dma((6,)), dma((Z,)), vmem((C + 2 * R, C), F32), dma, dma]
        + carried + carried,
        compiler_params=pltpu.CompilerParams(
            collective_id=0, has_side_effects=True, vmem_limit_bytes=60 * 1024 * 1024
        ),
    )(queries[0], key_vectors[0], value_vectors[0], log_decay[0], out_weight, cotangent[0])
    outs = pl.pallas_call(
        store,
        out_shape=[jax.ShapeDtypeStruct(shape, dtype) for shape, dtype in RESULTS],
        in_specs=[pl.BlockSpec(memory_space=pl.ANY)] * 5,
        out_specs=[pl.BlockSpec(memory_space=pl.ANY)] * 5,
        scratch_shapes=[dma((5,))],
        compiler_params=pltpu.CompilerParams(vmem_limit_bytes=1024 * 1024),
    )(*outs)
    return tuple(out[None] for out in outs[:4]) + (outs[4],)


def solution(mesh):
    rows = P("dp", "ctx", None)
    return jax.shard_map(
        body,
        mesh=mesh,
        in_specs=(rows, rows, rows, rows, P(), rows),
        out_specs=(rows, rows, rows, rows, P("dp", None)),
        check_vma=False,
    )
```

```python
import jax
import jax.numpy as jnp
from jax import lax
from jax.experimental import pallas as pl
from jax.experimental.pallas import tpu as pltpu
from jax.sharding import PartitionSpec as P

X, Y, Z, ZL, ZH = 4, 8, 12, 3, 4
T = 128
C = 128
D = 5120
R = D // (X * Y * ZH)
EPSILON = 1e-05
MESH = pl.DeviceIdType.MESH
F32 = jnp.float32
BF16 = jnp.bfloat16
RESULTS = [((T, C), BF16)] * 3 + [((T, C), F32), ((R, C), F32)]


def mm(a, b, dims=((1,), (0,)), precision=lax.Precision.HIGHEST):
    return lax.dot_general(a, b, (dims, ((), ())), precision=precision, preferred_element_type=F32)


NT = ((1,), (1,))
TN = ((0,), (0,))


class Ring:
    def __init__(self, me, count, device, own, streams, slots, send, recv):
        self.me, self.count, self.device, self.own = me, count, device, own
        self.slots, self.send, self.recv = slots, send, recv
        self.streams, base = [], 0
        for part, sign, hops in streams:
            self.streams.append((part, sign, hops, base))
            base += hops

    def dest(self, stream, turn):
        _, sign, hops, _ = self.streams[stream]
        return lax.rem(self.me + sign * (hops - turn) + self.count, self.count)

    def copy(self, stream, turn):
        part, sign, _, base = self.streams[stream]
        source = self.own(self.dest(stream, 0), part) if turn == 0 else self.slots.at[base + turn - 1]
        return pltpu.make_async_remote_copy(
            src_ref=source,
            dst_ref=self.slots.at[base + turn],
            send_sem=self.send.at[base + turn],
            recv_sem=self.recv.at[base + turn],
            device_id=self.device(sign),
            device_id_type=MESH,
        )

    def start(self, stream):
        self.copy(stream, 0).start()

    def step(self, stream, turn):
        part, _, _, base = self.streams[stream]
        self.copy(stream, turn - 1).wait_recv()
        self.slots[base + turn - 1] += self.own(self.dest(stream, turn), part)[...]
        self.copy(stream, turn).start()

    def finish(self, stream):
        part, _, hops, base = self.streams[stream]
        self.copy(stream, hops - 1).wait_recv()
        self.own(self.me, part)[...] += self.slots[base + hops - 1]

    def drain(self):
        for index, (_, _, hops, _) in enumerate(self.streams):
            for turn in range(hops):
                self.copy(index, turn).wait_send()


class Direct:
    def __init__(self, me, count, device, own, order, slots, send, recv):
        self.me, self.count, self.device, self.own, self.order = me, count, device, own, order
        self.slots, self.send, self.recv = slots, send, recv

    def copy(self, index):
        step = self.order[index]
        return pltpu.make_async_remote_copy(
            src_ref=self.own(lax.rem(self.me + step, self.count)),
            dst_ref=self.slots.at[index],
            send_sem=self.send.at[index],
            recv_sem=self.recv.at[index],
            device_id=self.device(step),
            device_id_type=MESH,
        )

    def start(self):
        for index in range(len(self.order)):
            self.copy(index).start()

    def finish(self):
        total = self.own(self.me)[...]
        for index in reversed(range(len(self.order))):
            self.copy(index).wait_recv()
            total += self.slots[index]
        self.own(self.me)[...] = total

    def drain(self):
        for index in range(len(self.order)):
            self.copy(index).wait_send()


def kernel(
    q_hbm, k_hbm, v_hbm, decay_hbm, weight_hbm, cot_hbm,
    gq_ref, gk_ref, gv_ref, gd_ref, gw_ref,
    q_in, k_in, v_in, decay_in, weight_in, cot_in, cot_t, in_sem,
    acc, pair_slots, pair_send, pair_recv,
    x1_slots, x1_send, x1_recv, y1_slots, y1_send, y1_recv, far_slots, far_send, far_recv,
    x2_slots, x2_send, x2_recv, y2_slots, y2_send, y2_recv,
    z_slots, z_send, z_recv, w_out, w_send, w_recv,
    f_loc, f_mate, f_pair, f_in, f_mate_send, f_mate_recv, f_send, f_recv,
    b_loc, b_mate, b_pair, b_in, b_mate_send, b_mate_recv, b_send, b_recv, y_here, z_here,
):
    dp, ctx = lax.axis_index("dp"), lax.axis_index("ctx")
    yy = dp // (X * ZH)
    xx = (dp // ZH) % X
    zz = (dp % ZH) * ZL + ctx // 2
    core = ctx % 2
    chip = ctx // 2

    def at(y, x, z, h):
        return {"dp": (y * X + x) * ZH + z // ZL, "ctx": (z % ZL) * 2 + h}

    def near_x(sign):
        return at(yy, lax.rem(xx + sign + X, X), zz, core)

    def near_y(sign):
        return at(lax.rem(yy + sign + Y, Y), xx, zz, core)

    mate = at(yy, xx, zz, 1 - core)
    base_z = 6 * core
    gathers = zz // 6 == core

    operands = (
        (decay_hbm, decay_in), (k_hbm, k_in), (v_hbm, v_in), (q_hbm, q_in), (cot_hbm, cot_in), (weight_hbm, weight_in),
    )
    loads = [pltpu.make_async_copy(a, b, in_sem.at[i]) for i, (a, b) in enumerate(operands)]
    for load in loads:
        load.start()

    barrier = pltpu.get_barrier_semaphore()

    def greet(device):
        pl.semaphore_signal(barrier, inc=1, device_id=device, device_id_type=MESH)

    for step in (3, 9, 2, 10, 1, 11):
        greet(at(yy, xx, lax.rem(zz + step, Z), core))
    for step in (2, 6, 1, 7):
        greet(near_y(step))
    for step in (2, 1, 3):
        greet(near_x(step))
    for step in range(1, 6):
        greet({"dp": dp, "ctx": lax.rem(ctx + step, 6)})

    row = lax.broadcasted_iota(jnp.int32, (T, T), 0)
    column = lax.broadcasted_iota(jnp.int32, (T, T), 1)
    lower = (row >= column).astype(F32)
    loads[0].wait()
    cumul = mm(lower, decay_in[...])
    total = cumul[T - 1 : T, :]
    decay = jnp.exp(total)
    loads[1].wait()
    loads[2].wait()
    key = k_in[...].astype(F32)
    value = v_in[...].astype(F32)
    key_to_end = key * jnp.exp(total - cumul)
    local = mm(value, key_to_end, TN)
    f_loc[:C, :] = local
    f_loc[C:, :] = jnp.broadcast_to(decay, (8, C))

    pl.semaphore_wait(barrier, 18)

    def relay(sem, device):
        pl.semaphore_signal(sem, inc=1, device_id=device, device_id_type=MESH)

    def far_sends(pair, slots, send, recv, first, last):
        def copy(slot, target, h, index):
            return pltpu.make_async_remote_copy(
                pair, slots.at[slot], send.at[index], recv.at[slot],
                device_id={"dp": dp, "ctx": 2 * target + h}, device_id_type=MESH,
            )

        from_first = [copy(0, last, h, h) for h in (0, 1)] + [copy(0, 1, h, 2 + h) for h in (0, 1)]
        from_middle = [copy(1, last, h, h) for h in (0, 1)]
        return from_first, from_middle

    f_first, f_middle = far_sends(f_pair, f_in, f_send, f_recv, 0, 2)
    b_first, b_middle = far_sends(b_pair, b_in, b_send, b_recv, 2, 0)
    f_to_mate = pltpu.make_async_remote_copy(
        f_loc, f_mate, f_mate_send, f_mate_recv, device_id=mate, device_id_type=MESH
    )
    b_to_mate = pltpu.make_async_remote_copy(
        b_loc, b_mate, b_mate_send, b_mate_recv, device_id=mate, device_id_type=MESH
    )
    even = core == 0
    odd = core == 1

    @pl.when(even)
    def _():
        f_to_mate.start()

    for step in (3, 9):
        relay(z_here, at(yy, xx, lax.rem(zz + step, Z), core))
    for step in (2, 6):
        relay(y_here, near_y(step))

    loads[3].wait()
    query = q_in[...].astype(F32)
    rising = jnp.exp(cumul)
    falling = jnp.exp(-cumul)
    query_scaled = query * rising
    key_scaled = key * falling
    scores = mm(query_scaled, key_scaled, NT) * lower

    @pl.when(odd)
    def _():
        f_to_mate.wait_recv()
        f_pair[:C, :] = f_loc[C : C + 1, :] * f_mate[:C, :] + f_loc[:C, :]
        f_pair[C:, :] = f_loc[C:, :] * f_mate[C:, :]

        @pl.when(chip == 0)
        def _():
            for copy in f_first:
                copy.start()

        @pl.when(chip == 1)
        def _():
            for copy in f_middle:
                copy.start()

    within = mm(scores, value)
    loads[4].wait()
    for i in range(D // 128):
        cot_t[128 * i : 128 * (i + 1), :] = cot_in[:, 128 * i : 128 * (i + 1)].T
    loads[5].wait()
    grad_normed = jnp.dot(cot_in[...], weight_in[...], preferred_element_type=F32)

    def carried(slots, copies_first, copies_middle, here_first, here_last, loc_in):
        @pl.when(chip == here_first)
        def _():
            loc_in[...] = jnp.zeros_like(loc_in)

        @pl.when(chip == 1)
        def _():
            copies_first[0].wait_recv()
            loc_in[...] = slots[0, :C, :]

        @pl.when(chip == here_last)
        def _():
            copies_first[0].wait_recv()
            copies_middle[0].wait_recv()
            loc_in[...] = slots[1, C : C + 1, :] * slots[0, :C, :] + slots[1, :C, :]

    state_ref = w_out.at[0:C]
    carried(f_in, f_first, f_middle, 0, 2, state_ref)

    @pl.when(odd)
    def _():
        state_ref[...] = f_mate[C : C + 1, :] * state_ref[...] + f_mate[:C, :]

    state_in = state_ref[...]
    output = within + mm(query_scaled, state_in, NT)
    scale_inv = lax.rsqrt(jnp.mean(output * output, axis=-1, keepdims=True) + EPSILON)
    normed = output * scale_inv
    rounded = normed.astype(BF16)

    mine, theirs = 2 * core, 2 * (1 - core)
    x_order = (2, 1, 3, 0)
    y_order = (3, 5, 4, 2, 6, 1, 7, 0)

    def x_pair(k):
        there = lax.rem(xx + x_order[k], X)
        return there, pltpu.make_async_remote_copy(
            acc.at[:, there, theirs],
            pair_slots.at[0, :, there],
            pair_send.at[k],
            pair_recv.at[k],
            device_id=mate,
            device_id_type=MESH,
        )

    def y_pair(k):
        there = lax.rem(yy + y_order[k], Y)
        return there, pltpu.make_async_remote_copy(
            acc.at[there, :, theirs + 1],
            pair_slots.at[1, there],
            pair_send.at[X + k],
            pair_recv.at[X + k],
            device_id=mate,
            device_id_type=MESH,
        )

    for k in range(Y):
        there, copy = y_pair(k)
        for x in range(X):
            rows = pl.ds(pl.multiple_of((there * X + x) * (ZH * R), 32), ZH * R)
            share = jnp.dot(cot_t[rows, :], rounded, preferred_element_type=F32)
            acc[there, x] = share.reshape(ZH, R, C)
        if k < 3:
            copy.start()
    halves = (("x", 0), ("x", 1), ("x", 2), ("y", 3), ("y", 4), ("x", 3)) + tuple(("y", k) for k in range(5, Y))
    for axis, k in halves:
        (x_pair if axis == "x" else y_pair)(k)[1].start()

    grad_output = scale_inv * (grad_normed - normed * jnp.mean(grad_normed * normed, axis=-1, keepdims=True))
    b_loc[:C, :] = mm(grad_output, query_scaled, TN)
    b_loc[C:, :] = jnp.broadcast_to(decay, (8, C))

    @pl.when(odd)
    def _():
        b_to_mate.start()

    x1 = Ring(
        xx, X, near_x, lambda dest, part: acc.at[4 * part : 4 * part + 4, dest, mine],
        ((0, 1, 2), (1, -1, 2), (1, 1, 1), (0, -1, 1)), x1_slots, x1_send, x1_recv,
    )
    y1 = Ring(
        yy, Y, near_y, lambda dest, part: acc.at[dest, 2 * part : 2 * part + 2, mine + 1],
        ((0, 1, 3), (0, -1, 3), (1, 1, 3), (1, -1, 3)), y1_slots, y1_send, y1_recv,
    )
    far_y = Direct(yy, Y, near_y, lambda dest: acc.at[dest, :, mine + 1], (4,), far_slots, far_send, far_recv)
    x2 = Direct(yy, Y, near_y, lambda dest: acc.at[dest, xx, mine], (4, 3, 5, 2, 6, 1, 7), x2_slots, x2_send, x2_recv)
    y2 = Direct(xx, X, near_x, lambda dest: acc.at[yy, dest, mine + 1], (2, 1, 3), y2_slots, y2_send, y2_recv)

    def take_x(k):
        there, copy = x_pair(k)
        copy.wait_recv()
        acc[:, there, mine] += pair_slots[0, :, there]

    def take_y(k):
        there, copy = y_pair(k)
        copy.wait_recv()
        acc[there, :, mine + 1] += pair_slots[1, there]

    take_y(0)
    y1.start(0)
    y1.start(2)
    take_y(1)
    y1.start(1)
    y1.start(3)
    take_x(0)
    x1.start(0)
    x1.start(1)
    take_x(1)
    x1.start(2)
    take_x(2)
    x1.start(3)
    take_y(2)
    pl.semaphore_wait(y_here, 2)
    far_y.start()
    take_x(3)
    for k in range(3, Y):
        take_y(k)

    @pl.when(even)
    def _():
        b_to_mate.wait_recv()
        b_pair[:C, :] = b_loc[C : C + 1, :] * b_mate[:C, :] + b_loc[:C, :]
        b_pair[C:, :] = b_loc[C:, :] * b_mate[C:, :]

        @pl.when(chip == 2)
        def _():
            for copy in b_first:
                copy.start()

        @pl.when(chip == 1)
        def _():
            for copy in b_middle:
                copy.start()

    y1.step(0, 1)
    y1.step(1, 1)
    x1.step(0, 1)
    x1.step(1, 1)
    y1.step(2, 1)
    y1.step(3, 1)
    pairs = mm(grad_output, value, NT) * lower
    y1.step(0, 2)
    y1.step(1, 2)
    grad_query = rising * (mm(pairs, key_scaled) + mm(grad_output, state_in))
    gq_ref[...] = grad_query.astype(BF16)
    y1.step(2, 2)
    y1.step(3, 2)
    for stream in (2, 3, 0, 1):
        x1.finish(stream)
    x2.start()
    grad_key = falling * mm(pairs, query_scaled, TN)
    for stream in (2, 3, 0, 1):
        y1.finish(stream)
    far_y.finish()
    y2.start()
    grad_value = mm(scores, grad_output, TN)

    later_ref = w_out.at[0:C]
    carried(b_in, b_first, b_middle, 2, 0, later_ref)

    @pl.when(even)
    def _():
        later_ref[...] = b_mate[C : C + 1, :] * later_ref[...] + b_mate[:C, :]

    later = later_ref[...]
    grad_key += jnp.exp(total - cumul) * mm(value, later)
    gk_ref[...] = grad_key.astype(BF16)
    x2.finish()

    def z_copy(i):
        part = 0 if i < ZL else 1
        return pltpu.make_async_remote_copy(
            acc.at[yy, xx, mine + part],
            z_slots.at[zz],
            z_send.at[i],
            z_recv.at[zz],
            device_id=at(yy, xx, base_z + i, core),
            device_id_type=MESH,
        )

    def z_each(which, act):
        for i in which:

            @pl.when(base_z + i != zz)
            def _():
                act(z_copy(i))

    pl.semaphore_wait(z_here, 2)
    z_each(range(ZL), lambda copy: copy.start())
    y2.finish()
    z_each(range(ZL, 2 * ZL), lambda copy: copy.start())

    grad_value += mm(key_to_end, later, NT)
    gv_ref[...] = grad_value.astype(BF16)
    gate = query * grad_query - key * grad_key
    end_state = local + decay * state_in
    later_sum = jnp.sum(end_state * later, axis=0, keepdims=True)
    gd_ref[...] = mm(lower, gate, TN) + later_sum

    to_mate = pltpu.make_async_remote_copy(
        w_out.at[C : C + R], w_out.at[C + R :], w_send, w_recv, device_id=mate, device_id_type=MESH
    )

    @pl.when(gathers)
    def _():
        z_slots[zz] = acc[yy, xx, zz // ZL]
        for i in range(Z):

            @pl.when(zz != i)
            def _():
                pltpu.make_async_remote_copy(
                    z_slots.at[i], z_slots.at[i], z_send.at[0], z_recv.at[i], device_id=mate, device_id_type=MESH
                ).wait_recv()

        summed = z_slots[0]
        for i in range(1, Z):
            summed += z_slots[i]
        w_out[C : C + R, :] = summed
        to_mate.start()
        gw_ref[...] = summed
        to_mate.wait_send()

    @pl.when(jnp.logical_not(gathers))
    def _():
        to_mate.wait_recv()
        gw_ref[...] = w_out[C + R :, :]

    z_each(range(2 * ZL), lambda copy: copy.wait_send())
    for k in range(X):
        x_pair(k)[1].wait_send()
    for k in range(Y):
        y_pair(k)[1].wait_send()
    for ring in (x1, y1, far_y, x2, y2):
        ring.drain()

    @pl.when(even)
    def _():
        f_to_mate.wait_send()

        @pl.when(chip == 2)
        def _():
            for copy in b_first:
                copy.wait_send()

        @pl.when(chip == 1)
        def _():
            for copy in b_middle:
                copy.wait_send()

    @pl.when(odd)
    def _():
        b_to_mate.wait_send()

        @pl.when(chip == 0)
        def _():
            for copy in f_first:
                copy.wait_send()

        @pl.when(chip == 1)
        def _():
            for copy in f_middle:
                copy.wait_send()


def store(*refs):
    copies = [pltpu.make_async_copy(refs[i], refs[5 + i], refs[10].at[i]) for i in range(5)]
    for copy in copies:
        copy.start()
    for copy in copies:
        copy.wait()


def body(queries, key_vectors, value_vectors, log_decay, out_weight, cotangent):
    vmem, dma = pltpu.VMEM, pltpu.SemaphoreType.DMA

    def slots(count, *block):
        return [vmem((count, *block, R, C), F32), dma((count,)), dma((count,))]

    carried = [vmem((C + 8, C), F32)] * 3 + [vmem((2, C + 8, C), F32), dma, dma, dma((4,)), dma((2,))]
    outs = pl.pallas_call(
        kernel,
        out_shape=[pltpu.VMEM(shape, dtype) for shape, dtype in RESULTS],
        in_specs=[pl.BlockSpec(memory_space=pltpu.HBM)] * 6,
        out_specs=[pl.BlockSpec(memory_space=pltpu.VMEM)] * 5,
        scratch_shapes=[vmem((T, C), BF16)] * 3
        + [vmem((T, C), F32), vmem((D, C), BF16), vmem((T, D), BF16), vmem((D, T), BF16), dma((6,))]
        + [vmem((Y, X, ZH, R, C), F32), vmem((2, Y, X, R, C), F32), dma((X + Y,)), dma((X + Y,))]
        + slots(6, 4) + slots(12, 2) + slots(1, X) + slots(7) + slots(3)
        + [vmem((Z, R, C), F32), dma((6,)), dma((Z,)), vmem((C + 2 * R, C), F32), dma, dma]
        + carried + carried + [pltpu.SemaphoreType.REGULAR] * 2,
        compiler_params=pltpu.CompilerParams(
            collective_id=0, has_side_effects=True, vmem_limit_bytes=60 * 1024 * 1024
        ),
    )(queries[0], key_vectors[0], value_vectors[0], log_decay[0], out_weight, cotangent[0])
    outs = pl.pallas_call(
        store,
        out_shape=[jax.ShapeDtypeStruct(shape, dtype) for shape, dtype in RESULTS],
        in_specs=[pl.BlockSpec(memory_space=pl.ANY)] * 5,
        out_specs=[pl.BlockSpec(memory_space=pl.ANY)] * 5,
        scratch_shapes=[dma((5,))],
        compiler_params=pltpu.CompilerParams(vmem_limit_bytes=1024 * 1024),
    )(*outs)
    return tuple(out[None] for out in outs[:4]) + (outs[4],)


def solution(mesh):
    rows = P("dp", "ctx", None)
    return jax.shard_map(
        body,
        mesh=mesh,
        in_specs=(rows, rows, rows, rows, P(), rows),
        out_specs=(rows, rows, rows, rows, P("dp", None)),
        check_vma=False,
    )
```

```python
import jax
import jax.numpy as jnp
from jax import lax
from jax.experimental import pallas as pl
from jax.experimental.pallas import tpu as pltpu
from jax.sharding import PartitionSpec as P

X, Y, Z, ZL, ZH = 4, 8, 12, 3, 4
T = 128
C = 128
D = 5120
R = D // (X * Y * ZH)
EPSILON = 1e-05
MESH = pl.DeviceIdType.MESH
F32 = jnp.float32
BF16 = jnp.bfloat16
RESULTS = [((T, C), BF16)] * 3 + [((T, C), F32), ((R, C), F32)]


def mm(a, b, dims=((1,), (0,)), precision=lax.Precision.HIGHEST):
    return lax.dot_general(a, b, (dims, ((), ())), precision=precision, preferred_element_type=F32)


NT = ((1,), (1,))
TN = ((0,), (0,))


class Ring:
    def __init__(self, me, count, device, own, streams, slots, send, recv):
        self.me, self.count, self.device, self.own = me, count, device, own
        self.slots, self.send, self.recv = slots, send, recv
        self.streams, base = [], 0
        for part, sign, hops in streams:
            self.streams.append((part, sign, hops, base))
            base += hops

    def dest(self, stream, turn):
        _, sign, hops, _ = self.streams[stream]
        return lax.rem(self.me + sign * (hops - turn) + self.count, self.count)

    def copy(self, stream, turn):
        part, sign, _, base = self.streams[stream]
        source = self.own(self.dest(stream, 0), part) if turn == 0 else self.slots.at[base + turn - 1]
        return pltpu.make_async_remote_copy(
            src_ref=source,
            dst_ref=self.slots.at[base + turn],
            send_sem=self.send.at[base + turn],
            recv_sem=self.recv.at[base + turn],
            device_id=self.device(sign),
            device_id_type=MESH,
        )

    def start(self, stream):
        self.copy(stream, 0).start()

    def step(self, stream, turn):
        part, _, _, base = self.streams[stream]
        self.copy(stream, turn - 1).wait_recv()
        self.slots[base + turn - 1] += self.own(self.dest(stream, turn), part)[...]
        self.copy(stream, turn).start()

    def finish(self, stream):
        part, _, hops, base = self.streams[stream]
        self.copy(stream, hops - 1).wait_recv()
        self.own(self.me, part)[...] += self.slots[base + hops - 1]

    def drain(self):
        for index, (_, _, hops, _) in enumerate(self.streams):
            for turn in range(hops):
                self.copy(index, turn).wait_send()


class Direct:
    def __init__(self, me, count, device, own, order, slots, send, recv):
        self.me, self.count, self.device, self.own, self.order = me, count, device, own, order
        self.slots, self.send, self.recv = slots, send, recv

    def copy(self, index):
        step = self.order[index]
        return pltpu.make_async_remote_copy(
            src_ref=self.own(lax.rem(self.me + step, self.count)),
            dst_ref=self.slots.at[index],
            send_sem=self.send.at[index],
            recv_sem=self.recv.at[index],
            device_id=self.device(step),
            device_id_type=MESH,
        )

    def start(self):
        for index in range(len(self.order)):
            self.copy(index).start()

    def finish(self):
        total = self.own(self.me)[...]
        for index in reversed(range(len(self.order))):
            self.copy(index).wait_recv()
            total += self.slots[index]
        self.own(self.me)[...] = total

    def drain(self):
        for index in range(len(self.order)):
            self.copy(index).wait_send()


def kernel(
    q_hbm, k_hbm, v_hbm, decay_hbm, weight_hbm, cot_hbm,
    gq_ref, gk_ref, gv_ref, gd_ref, gw_ref,
    q_in, k_in, v_in, decay_in, weight_in, cot_in, cot_t, in_sem,
    acc, pair_slots, pair_send, pair_recv,
    x1_slots, x1_send, x1_recv, y1_slots, y1_send, y1_recv, far_slots, far_send, far_recv,
    x2_slots, x2_send, x2_recv, y2_slots, y2_send, y2_recv,
    z_slots, z_send, z_recv, w_out, w_send, w_recv,
    f_loc, f_mate, f_pair, f_in, f_mate_send, f_mate_recv, f_send, f_recv,
    b_loc, b_mate, b_pair, b_in, b_mate_send, b_mate_recv, b_send, b_recv, y_here, z_here,
):
    dp, ctx = lax.axis_index("dp"), lax.axis_index("ctx")
    yy = dp // (X * ZH)
    xx = (dp // ZH) % X
    zz = (dp % ZH) * ZL + ctx // 2
    core = ctx % 2
    chip = ctx // 2

    def at(y, x, z, h):
        return {"dp": (y * X + x) * ZH + z // ZL, "ctx": (z % ZL) * 2 + h}

    def near_x(sign):
        return at(yy, lax.rem(xx + sign + X, X), zz, core)

    def near_y(sign):
        return at(lax.rem(yy + sign + Y, Y), xx, zz, core)

    mate = at(yy, xx, zz, 1 - core)
    base_z = 6 * core
    gathers = zz // 6 == core

    operands = (
        (decay_hbm, decay_in), (k_hbm, k_in), (v_hbm, v_in), (q_hbm, q_in), (cot_hbm, cot_in), (weight_hbm, weight_in),
    )
    loads = [pltpu.make_async_copy(a, b, in_sem.at[i]) for i, (a, b) in enumerate(operands)]
    for load in loads:
        load.start()

    barrier = pltpu.get_barrier_semaphore()

    def greet(device):
        pl.semaphore_signal(barrier, inc=1, device_id=device, device_id_type=MESH)

    for step in (3, 9, 2, 10, 1, 11):
        greet(at(yy, xx, lax.rem(zz + step, Z), core))
    for step in (2, 6, 1, 7):
        greet(near_y(step))
    for step in (2, 1, 3):
        greet(near_x(step))
    for step in range(1, 6):
        greet({"dp": dp, "ctx": lax.rem(ctx + step, 6)})

    row = lax.broadcasted_iota(jnp.int32, (T, T), 0)
    column = lax.broadcasted_iota(jnp.int32, (T, T), 1)
    lower = (row >= column).astype(F32)
    loads[0].wait()
    cumul = mm(lower, decay_in[...])
    total = cumul[T - 1 : T, :]
    decay = jnp.exp(total)
    loads[1].wait()
    loads[2].wait()
    key = k_in[...].astype(F32)
    value = v_in[...].astype(F32)
    key_to_end = key * jnp.exp(total - cumul)
    local = mm(value, key_to_end, TN)
    f_loc[:C, :] = local
    f_loc[C:, :] = jnp.broadcast_to(decay, (8, C))

    pl.semaphore_wait(barrier, 18)

    def relay(sem, device):
        pl.semaphore_signal(sem, inc=1, device_id=device, device_id_type=MESH)

    def far_sends(pair, slots, send, recv, first, last):
        def copy(slot, target, h, index):
            return pltpu.make_async_remote_copy(
                pair, slots.at[slot], send.at[index], recv.at[slot],
                device_id={"dp": dp, "ctx": 2 * target + h}, device_id_type=MESH,
            )

        from_first = [copy(0, last, h, h) for h in (0, 1)] + [copy(0, 1, h, 2 + h) for h in (0, 1)]
        from_middle = [copy(1, last, h, h) for h in (0, 1)]
        return from_first, from_middle

    def f_onward(slot, target, index):
        return pltpu.make_async_remote_copy(
            f_pair, f_in.at[slot], f_send.at[index], f_recv.at[slot],
            device_id={"dp": dp, "ctx": 2 * target + core}, device_id_type=MESH,
        )

    f_first, f_middle = [f_onward(0, 2, 0), f_onward(0, 1, 1)], [f_onward(1, 2, 0)]
    b_first, b_middle = far_sends(b_pair, b_in, b_send, b_recv, 2, 0)
    f_to_mate = pltpu.make_async_remote_copy(
        f_loc, f_mate, f_mate_send, f_mate_recv, device_id=mate, device_id_type=MESH
    )
    b_to_mate = pltpu.make_async_remote_copy(
        b_loc, b_mate, b_mate_send, b_mate_recv, device_id=mate, device_id_type=MESH
    )
    even = core == 0
    odd = core == 1

    f_to_mate.start()

    for step in (3, 9):
        relay(z_here, at(yy, xx, lax.rem(zz + step, Z), core))
    for step in (2, 6):
        relay(y_here, near_y(step))

    loads[3].wait()
    query = q_in[...].astype(F32)
    rising = jnp.exp(cumul)
    falling = jnp.exp(-cumul)
    query_scaled = query * rising
    key_scaled = key * falling
    scores = mm(query_scaled, key_scaled, NT) * lower

    f_to_mate.wait_recv()

    @pl.when(odd)
    def _():
        f_pair[:C, :] = f_loc[C : C + 1, :] * f_mate[:C, :] + f_loc[:C, :]

    @pl.when(even)
    def _():
        f_pair[:C, :] = f_mate[C : C + 1, :] * f_loc[:C, :] + f_mate[:C, :]

    f_pair[C:, :] = f_loc[C:, :] * f_mate[C:, :]

    @pl.when(chip == 0)
    def _():
        for copy in f_first:
            copy.start()

    @pl.when(chip == 1)
    def _():
        for copy in f_middle:
            copy.start()

    within = mm(scores, value)
    loads[4].wait()
    for i in range(D // 128):
        cot_t[128 * i : 128 * (i + 1), :] = cot_in[:, 128 * i : 128 * (i + 1)].T
    loads[5].wait()
    grad_normed = jnp.dot(cot_in[...], weight_in[...], preferred_element_type=F32)

    def carried(slots, copies_first, copies_middle, here_first, here_last, loc_in):
        @pl.when(chip == here_first)
        def _():
            loc_in[...] = jnp.zeros_like(loc_in)

        @pl.when(chip == 1)
        def _():
            copies_first[0].wait_recv()
            loc_in[...] = slots[0, :C, :]

        @pl.when(chip == here_last)
        def _():
            copies_first[0].wait_recv()
            copies_middle[0].wait_recv()
            loc_in[...] = slots[1, C : C + 1, :] * slots[0, :C, :] + slots[1, :C, :]

    state_ref = w_out.at[0:C]
    carried(f_in, f_first, f_middle, 0, 2, state_ref)

    @pl.when(odd)
    def _():
        state_ref[...] = f_mate[C : C + 1, :] * state_ref[...] + f_mate[:C, :]

    state_in = state_ref[...]
    output = within + mm(query_scaled, state_in, NT)
    scale_inv = lax.rsqrt(jnp.mean(output * output, axis=-1, keepdims=True) + EPSILON)
    normed = output * scale_inv
    rounded = normed.astype(BF16)

    mine, theirs = 2 * core, 2 * (1 - core)
    x_order = (2, 1, 3, 0)
    y_order = (3, 5, 4, 2, 6, 1, 7, 0)

    def x_pair(k):
        there = lax.rem(xx + x_order[k], X)
        return there, pltpu.make_async_remote_copy(
            acc.at[:, there, theirs],
            pair_slots.at[0, :, there],
            pair_send.at[k],
            pair_recv.at[k],
            device_id=mate,
            device_id_type=MESH,
        )

    def y_pair(k):
        there = lax.rem(yy + y_order[k], Y)
        return there, pltpu.make_async_remote_copy(
            acc.at[there, :, theirs + 1],
            pair_slots.at[1, there],
            pair_send.at[X + k],
            pair_recv.at[X + k],
            device_id=mate,
            device_id_type=MESH,
        )

    for k in range(Y):
        there, copy = y_pair(k)
        for x in range(X):
            rows = pl.ds(pl.multiple_of((there * X + x) * (ZH * R), 32), ZH * R)
            share = jnp.dot(cot_t[rows, :], rounded, preferred_element_type=F32)
            acc[there, x] = share.reshape(ZH, R, C)
        if k < 3:
            copy.start()
    halves = (("x", 0), ("x", 1), ("x", 2), ("y", 3), ("y", 4), ("x", 3)) + tuple(("y", k) for k in range(5, Y))
    for axis, k in halves:
        (x_pair if axis == "x" else y_pair)(k)[1].start()

    grad_output = scale_inv * (grad_normed - normed * jnp.mean(grad_normed * normed, axis=-1, keepdims=True))
    b_loc[:C, :] = mm(grad_output, query_scaled, TN)
    b_loc[C:, :] = jnp.broadcast_to(decay, (8, C))

    @pl.when(odd)
    def _():
        b_to_mate.start()

    x1 = Ring(
        xx, X, near_x, lambda dest, part: acc.at[4 * part : 4 * part + 4, dest, mine],
        ((0, 1, 2), (1, -1, 2), (1, 1, 1), (0, -1, 1)), x1_slots, x1_send, x1_recv,
    )
    y1 = Ring(
        yy, Y, near_y, lambda dest, part: acc.at[dest, 2 * part : 2 * part + 2, mine + 1],
        ((0, 1, 3), (0, -1, 3), (1, 1, 3), (1, -1, 3)), y1_slots, y1_send, y1_recv,
    )
    far_y = Direct(yy, Y, near_y, lambda dest: acc.at[dest, :, mine + 1], (4,), far_slots, far_send, far_recv)
    x2 = Direct(yy, Y, near_y, lambda dest: acc.at[dest, xx, mine], (4, 3, 5, 2, 6, 1, 7), x2_slots, x2_send, x2_recv)
    y2 = Direct(xx, X, near_x, lambda dest: acc.at[yy, dest, mine + 1], (2, 1, 3), y2_slots, y2_send, y2_recv)

    def take_x(k):
        there, copy = x_pair(k)
        copy.wait_recv()
        acc[:, there, mine] += pair_slots[0, :, there]

    def take_y(k):
        there, copy = y_pair(k)
        copy.wait_recv()
        acc[there, :, mine + 1] += pair_slots[1, there]

    take_y(0)
    y1.start(0)
    y1.start(2)
    take_y(1)
    y1.start(1)
    y1.start(3)
    take_x(0)
    x1.start(0)
    x1.start(1)
    take_x(1)
    x1.start(2)
    take_x(2)
    x1.start(3)
    take_y(2)
    pl.semaphore_wait(y_here, 2)
    far_y.start()
    take_x(3)
    for k in range(3, Y):
        take_y(k)

    @pl.when(even)
    def _():
        b_to_mate.wait_recv()
        b_pair[:C, :] = b_loc[C : C + 1, :] * b_mate[:C, :] + b_loc[:C, :]
        b_pair[C:, :] = b_loc[C:, :] * b_mate[C:, :]

        @pl.when(chip == 2)
        def _():
            for copy in b_first:
                copy.start()

        @pl.when(chip == 1)
        def _():
            for copy in b_middle:
                copy.start()

    y1.step(0, 1)
    y1.step(1, 1)
    x1.step(0, 1)
    x1.step(1, 1)
    y1.step(2, 1)
    y1.step(3, 1)
    pairs = mm(grad_output, value, NT) * lower
    y1.step(0, 2)
    y1.step(1, 2)
    grad_query = rising * (mm(pairs, key_scaled) + mm(grad_output, state_in))
    gq_ref[...] = grad_query.astype(BF16)
    y1.step(2, 2)
    y1.step(3, 2)
    for stream in (2, 3, 0, 1):
        x1.finish(stream)
    x2.start()
    grad_key = falling * mm(pairs, query_scaled, TN)
    for stream in (2, 3, 0, 1):
        y1.finish(stream)
    far_y.finish()
    y2.start()
    grad_value = mm(scores, grad_output, TN)

    later_ref = w_out.at[0:C]
    carried(b_in, b_first, b_middle, 2, 0, later_ref)

    @pl.when(even)
    def _():
        later_ref[...] = b_mate[C : C + 1, :] * later_ref[...] + b_mate[:C, :]

    later = later_ref[...]
    grad_key += jnp.exp(total - cumul) * mm(value, later)
    gk_ref[...] = grad_key.astype(BF16)
    x2.finish()

    def z_copy(i):
        part = 0 if i < ZL else 1
        return pltpu.make_async_remote_copy(
            acc.at[yy, xx, mine + part],
            z_slots.at[zz],
            z_send.at[i],
            z_recv.at[zz],
            device_id=at(yy, xx, base_z + i, core),
            device_id_type=MESH,
        )

    def z_each(which, act):
        for i in which:

            @pl.when(base_z + i != zz)
            def _():
                act(z_copy(i))

    pl.semaphore_wait(z_here, 2)
    z_each(range(ZL), lambda copy: copy.start())
    y2.finish()
    z_each(range(ZL, 2 * ZL), lambda copy: copy.start())

    grad_value += mm(key_to_end, later, NT)
    gv_ref[...] = grad_value.astype(BF16)
    gate = query * grad_query - key * grad_key
    end_state = local + decay * state_in
    later_sum = jnp.sum(end_state * later, axis=0, keepdims=True)
    gd_ref[...] = mm(lower, gate, TN) + later_sum

    to_mate = pltpu.make_async_remote_copy(
        w_out.at[C : C + R], w_out.at[C + R :], w_send, w_recv, device_id=mate, device_id_type=MESH
    )

    @pl.when(gathers)
    def _():
        z_slots[zz] = acc[yy, xx, zz // ZL]
        for i in range(Z):

            @pl.when(zz != i)
            def _():
                pltpu.make_async_remote_copy(
                    z_slots.at[i], z_slots.at[i], z_send.at[0], z_recv.at[i], device_id=mate, device_id_type=MESH
                ).wait_recv()

        summed = z_slots[0]
        for i in range(1, Z):
            summed += z_slots[i]
        w_out[C : C + R, :] = summed
        to_mate.start()
        gw_ref[...] = summed
        to_mate.wait_send()

    @pl.when(jnp.logical_not(gathers))
    def _():
        to_mate.wait_recv()
        gw_ref[...] = w_out[C + R :, :]

    z_each(range(2 * ZL), lambda copy: copy.wait_send())
    for k in range(X):
        x_pair(k)[1].wait_send()
    for k in range(Y):
        y_pair(k)[1].wait_send()
    for ring in (x1, y1, far_y, x2, y2):
        ring.drain()

    @pl.when(even)
    def _():
        @pl.when(chip == 2)
        def _():
            for copy in b_first:
                copy.wait_send()

        @pl.when(chip == 1)
        def _():
            for copy in b_middle:
                copy.wait_send()

    @pl.when(odd)
    def _():
        b_to_mate.wait_send()

    f_to_mate.wait_send()

    @pl.when(chip == 0)
    def _():
        for copy in f_first:
            copy.wait_send()

    @pl.when(chip == 1)
    def _():
        for copy in f_middle:
            copy.wait_send()


def store(*refs):
    copies = [pltpu.make_async_copy(refs[i], refs[5 + i], refs[10].at[i]) for i in range(5)]
    for copy in copies:
        copy.start()
    for copy in copies:
        copy.wait()


def body(queries, key_vectors, value_vectors, log_decay, out_weight, cotangent):
    vmem, dma = pltpu.VMEM, pltpu.SemaphoreType.DMA

    def slots(count, *block):
        return [vmem((count, *block, R, C), F32), dma((count,)), dma((count,))]

    carried = [vmem((C + 8, C), F32)] * 3 + [vmem((2, C + 8, C), F32), dma, dma, dma((4,)), dma((2,))]
    outs = pl.pallas_call(
        kernel,
        out_shape=[pltpu.VMEM(shape, dtype) for shape, dtype in RESULTS],
        in_specs=[pl.BlockSpec(memory_space=pltpu.HBM)] * 6,
        out_specs=[pl.BlockSpec(memory_space=pltpu.VMEM)] * 5,
        scratch_shapes=[vmem((T, C), BF16)] * 3
        + [vmem((T, C), F32), vmem((D, C), BF16), vmem((T, D), BF16), vmem((D, T), BF16), dma((6,))]
        + [vmem((Y, X, ZH, R, C), F32), vmem((2, Y, X, R, C), F32), dma((X + Y,)), dma((X + Y,))]
        + slots(6, 4) + slots(12, 2) + slots(1, X) + slots(7) + slots(3)
        + [vmem((Z, R, C), F32), dma((6,)), dma((Z,)), vmem((C + 2 * R, C), F32), dma, dma]
        + carried + carried + [pltpu.SemaphoreType.REGULAR] * 2,
        compiler_params=pltpu.CompilerParams(
            collective_id=0, has_side_effects=True, vmem_limit_bytes=60 * 1024 * 1024
        ),
    )(queries[0], key_vectors[0], value_vectors[0], log_decay[0], out_weight, cotangent[0])
    outs = pl.pallas_call(
        store,
        out_shape=[jax.ShapeDtypeStruct(shape, dtype) for shape, dtype in RESULTS],
        in_specs=[pl.BlockSpec(memory_space=pl.ANY)] * 5,
        out_specs=[pl.BlockSpec(memory_space=pl.ANY)] * 5,
        scratch_shapes=[dma((5,))],
        compiler_params=pltpu.CompilerParams(vmem_limit_bytes=1024 * 1024),
    )(*outs)
    return tuple(out[None] for out in outs[:4]) + (outs[4],)


def solution(mesh):
    rows = P("dp", "ctx", None)
    return jax.shard_map(
        body,
        mesh=mesh,
        in_specs=(rows, rows, rows, rows, P(), rows),
        out_specs=(rows, rows, rows, rows, P("dp", None)),
        check_vma=False,
    )
```
